256 devices in a mesh: row: 32 (over z, y), col: 8 (over x, core).
Axes of the slice: x: 4, y: 4, z: 8, core: 2. Of those that a mesh axis runs over, the one named last changes fastest.
Arguments:
- coeffs: float32 [131072, 4096], P('row', 'col'), may hold values from -0.3125 to 0.3125
- pattern: int32 [2048, 64], P('row', 'col'), may hold values from 0 to 1, as said below
Outputs:
- band: float32 [256, 3, 512, 512], P(('row', 'col'))
The draws below stay inside these ranges and needn't reach their ends.
Inputs may be any that keep to these rules, and one draw needn't show every extreme that they name: Orbital locality: with c = (a * 64) // 2048, pattern[a, b] is 0 unless the circular distance min((b - c) mod 64, (c - b) mod 64) is at most 4. Some block row keeps a block at distance exactly 4 (where 64 allows it); no other structure is promised.
All inputs are finite; a program needn't handle non-finite values.
Results may differ from the reference program's by a relative error of at most 0.0003.
Values sent between devices are 32-bit elements; how exact they have to be, the bound alone decides.
No kernel may reach another device: no remote copies, remote signals or barrier semaphores. Data moves between devices by JAX's collectives and lax.ppermute only.
A program may use at most 128 MiB of HBM per device.

```python
import jax
import jax.numpy as jnp
from jax import lax

BLOCK = 64
R_SUB = 512
STEPS = 3
BASIS = 131072
ORBITALS = 4096
NSUB = 256
NBR = 2048
NBO = 64


def draw_pattern(key, part):
    local_key = jax.random.fold_in(key, 7)
    reach_key, keep_key, special_key = jax.random.split(local_key, 3)
    block_rows = jnp.arange(NBR, dtype=jnp.int32)
    block_cols = jnp.arange(NBO, dtype=jnp.int32)
    center = block_rows * NBO // NBR
    reach = jax.random.randint(reach_key, (NBR,), 1, 5, dtype=jnp.int32)
    special = jax.random.randint(special_key, (), 0, NBR, dtype=jnp.int32)
    reach = jnp.where(block_rows == special, 4, reach)
    offset = (block_cols[None, :] - center[:, None]) % NBO
    offset = jnp.minimum(offset, NBO - offset)
    keep = jax.random.randint(keep_key, (NBR, NBO), 0, 4, dtype=jnp.int32) < 3
    edge = block_cols[None, :] == ((center + reach) % NBO)[:, None]
    keep = jnp.logical_or(keep, edge)
    return jnp.logical_and(offset <= reach[:, None], keep).astype(jnp.int32)


def steps_of(key, extent, shards, smallest, top_value):
    factor_of, own = 1.0, jax.random.fold_in(key, 6)
    for dim, shards_of in shards:
        draws = jnp.exp(jax.random.uniform(jax.random.fold_in(own, dim), (shards_of,), jnp.float32, smallest / len(shards), top_value / len(shards)))
        factor_of = factor_of * jnp.repeat(draws, extent[dim] // shards_of).reshape([-1 if axis == dim else 1 for axis in range(len(extent))])
    return factor_of


def gaussian(own_key, shape, scale, most, pieces=(), kind=jnp.bfloat16):
    drawn = jax.random.normal(own_key, shape, jnp.float32) * scale
    if len(pieces) > 0:
        drawn = steps_of(own_key, shape, pieces, -0.22, 0.18) * drawn
    return jnp.clip(drawn, min=-most, max=most).astype(kind)


def setup_inputs(seed: int = 0) -> dict:
    splits = jax.random.split(jax.random.key(seed), 3)
    coeffs = gaussian(splits[0], (BASIS, ORBITALS), (max(ORBITALS // 12, BLOCK)) ** -0.5, 0.3125, ((0, 32), (1, 8)), jnp.float32)
    pattern = draw_pattern(jax.random.fold_in(splits[2], 71), 0)
    return dict(coeffs=coeffs, pattern=pattern)


def reference(coeffs, pattern):
    shaped = coeffs.reshape(NBR, BLOCK, NBO, BLOCK)
    masked = (shaped * pattern.astype(jnp.float32)[:, None, :, None]).reshape(NSUB, R_SUB, ORBITALS)
    offsets = jnp.arange(STEPS, dtype=jnp.int32)

    def one_block(index):
        picks = ((index + offsets) % NSUB).astype(jnp.int32)
        near = masked[picks].reshape(STEPS * R_SUB, ORBITALS)
        own = masked[index]
        product = jnp.dot(own, near.T, precision=lax.Precision.HIGHEST, preferred_element_type=jnp.float32)
        return product.reshape(R_SUB, STEPS, R_SUB).transpose(1, 0, 2)

    return lax.map(one_block, jnp.arange(NSUB, dtype=jnp.int32))
```

```python
import functools

import jax
import jax.numpy as jnp
from jax import lax
from jax.experimental import pallas as pl
from jax.experimental.pallas import tpu as pltpu
from jax.sharding import PartitionSpec as P


BLOCK = 64
SUB = 512
UNIT = 128
PAIR = 2 * SUB
STEPS = 3
ROWS, COLS, CHIPS, YS = 32, 8, 4, 4
SLOTS = 5


def device(r, x, c):
    return (r % ROWS) * COLS + (x % CHIPS) * 2 + c


def home(r):
    return (r // YS) // 2


def main_of(r):
    z = r // YS
    return device(r, z // 2, z % 2)


def side_of(r):
    z, y = r // YS, r % YS
    k = (z - 1 if y < 2 else z + 1) % COLS
    return device(r, k // 2, k % 2)


def tail_of(r):
    return main_of(r) if r % YS in (1, 2) else side_of(r)


def own(r, p):
    return device(r, p % CHIPS, 0)


def before(r, p):
    p = p % CHIPS
    return device(r, p - 1, 1) if p else device(r - 1, CHIPS - 1, 1)


def routes(source):
    groups = range(ROWS)
    return {
        "r1": (2, [(source(r), before(r, home(r) + 2)) for r in groups]),
        "l1": (3, [(source(r), own(r, home(r) + 3)) for r in groups]),
        "r2": (1, [(source(r), own(r, home(r) + 1)) for r in groups]),
        "l2": (0, [(source(r), before(r, home(r))) for r in groups]),
        "a0": (0, [(source(r), own(r, home(r))) for r in groups]),
        "a1": (1, [(source(r), before(r, home(r) + 1)) for r in groups]),
        "f1": (2, [(before(r, home(r) + 2), own(r, home(r) + 2)) for r in groups]),
        "f2": (3, [(own(r, home(r) + 3), before(r, home(r) + 3)) for r in groups]),
    }


ORDER = ("a0", "r2", "f1", "l1", "l2", "a1", "r1", "f2")


def place():
    r, k = lax.axis_index("row"), lax.axis_index("col")
    return r, r // YS, r % YS, k // 2, k % 2


def pick(index, values):
    out = jnp.int32(values[-1])
    for i, v in enumerate(values[:-1]):
        out = jnp.where(index == i, jnp.int32(v), out)
    return out


def pack_kernel(pairs, unit_by_y, width, has_extra, coeffs, pattern, *rest):
    extra, (out, buf, sems) = (rest[0], rest[1:]) if has_extra else (None, rest)
    _, z, y, _, _ = place()
    unit = pick(y, unit_by_y)
    chunk = 256
    per_pair = PAIR // chunk
    count = len(pairs) * per_pair

    def copy(i):
        pair = (z // 2 + pairs[i // per_pair]) % CHIPS
        row = pl.multiple_of(pair * PAIR + (i % per_pair) * chunk, chunk)
        return pltpu.make_async_copy(
            coeffs.at[pl.ds(row, chunk), pl.ds(pl.multiple_of(unit * UNIT, UNIT), width)],
            buf.at[pl.ds(i * chunk, chunk), :],
            sems.at[i],
        )

    for i in range(count):
        copy(i).start()
    lanes = lax.broadcasted_iota(jnp.int32, (COLS, width), 1) // BLOCK
    blocks = lax.broadcasted_iota(jnp.int32, (COLS, width), 0)
    spread = (blocks == lanes + 2 * unit).astype(jnp.float32)
    for n, p in enumerate(pairs):
        pair = (z // 2 + p) % CHIPS
        heights = PAIR // BLOCK
        kept = pattern[pl.ds(pl.multiple_of(pair * heights, heights), heights), :]
        mask = jnp.dot(kept.astype(jnp.float32), spread, preferred_element_type=jnp.float32)
        for i in range(n * per_pair, (n + 1) * per_pair):
            copy(i).wait()
            for b in range(chunk // BLOCK):
                rows = pl.ds(i * chunk + b * BLOCK, BLOCK)
                line = (i - n * per_pair) * (chunk // BLOCK) + b
                value = buf[rows, :] * mask[line : line + 1, :]
                if has_extra:
                    inner = jnp.logical_or(y == 1, y == 2)
                    first = jnp.where(inner, extra[rows, :], value[:, :UNIT])
                    out[rows, :UNIT] = first
                    out[rows, UNIT:] = value[:, UNIT:]
                else:
                    out[rows, :] = value


def pack(coeffs, pattern, pairs, unit_by_y, width, extra=None):
    height = len(pairs) * PAIR
    vmem = pl.BlockSpec(memory_space=pltpu.VMEM)
    args = (coeffs, pattern) + (() if extra is None else (extra,))
    return pl.pallas_call(
        functools.partial(pack_kernel, pairs, unit_by_y, width, extra is not None),
        out_shape=jax.ShapeDtypeStruct((height, width), jnp.float32),
        in_specs=[pl.BlockSpec(memory_space=pl.ANY), vmem] + [vmem] * (extra is not None),
        out_specs=vmem,
        scratch_shapes=[
            pltpu.VMEM((height, width), jnp.float32),
            pltpu.SemaphoreType.DMA((height // 256,)),
        ],
    )(*args)


def role_here():
    r, z, y, x, c = place()
    far = jnp.logical_and(c == 1, x == CHIPS - 1)
    group = jnp.where(far, (r + 1) % ROWS, r)
    pair = (x + c) % CHIPS
    return c * CHIPS + (pair - group // YS // 2) % CHIPS


def half_kernel(*refs):
    mains, tails, (out, sems) = refs[:8], refs[8:16], refs[16:]
    role = role_here()
    for n in range(8):
        @pl.when(role == n)
        def _():
            rows = pl.ds(SUB if n < CHIPS else 0, SUB)
            a = pltpu.make_async_copy(mains[n].at[rows, :], out.at[:, pl.ds(0, 3 * UNIT)], sems.at[0])
            b = pltpu.make_async_copy(tails[n].at[rows, :], out.at[:, pl.ds(3 * UNIT, 2 * UNIT)], sems.at[1])
            a.start()
            b.start()
            a.wait()
            b.wait()


def half(mains, tails):
    hbm = pl.BlockSpec(memory_space=pl.ANY)
    return pl.pallas_call(
        half_kernel,
        out_shape=jax.ShapeDtypeStruct((SUB, SLOTS * UNIT), jnp.float32),
        in_specs=[hbm] * 16,
        out_specs=hbm,
        scratch_shapes=[pltpu.SemaphoreType.DMA((2,))],
    )(*mains, *tails)


SLOT = ((2, 3, 4, 0, 1), (1, 2, 3, 0, 4), (0, 1, 2, 4, 3), (0, 1, 2, 3, 4))
BF = jnp.bfloat16


def band_kernel(*refs):
    mains, tails, swapped = refs[:8], refs[8:16], refs[16]
    out, full, high, low, sems = refs[17:]
    r, z, y, x, c = place()
    role = role_here()
    last = x == CHIPS - 1
    later = (y + 1) % YS

    def dot(a, b):
        return lax.dot_general(a, b, (((1,), (1,)), ((), ())), preferred_element_type=jnp.float32)

    def column(shifted, unit):
        here = pick(y, [s[unit] for s in SLOT])
        there = pick(later, [s[unit] for s in SLOT]) + 1
        return jnp.where(shifted, there, here)

    def put(source, rows, unit, col, block, shifted, sem):
        col = jnp.where(col > SLOTS - 1, SLOTS, col)
        return pltpu.make_async_copy(
            source.at[rows, pl.ds(unit * UNIT, UNIT)],
            full.at[col, pl.ds(pl.multiple_of(block * SUB, SUB), SUB), :],
            sem,
        )

    pair_shifted = jnp.logical_and(last, c == 1)
    swap_shifted = jnp.logical_and(last, c == 0)

    def copies(n):
        made = []
        for j in range(2):
            rows = pl.ds(j * SUB, SUB)
            for u in range(SLOTS):
                source = mains[n] if u < 3 else tails[n]
                at = u if u < 3 else u - 3
                made.append(put(source, rows, at, column(pair_shifted, u), c + j, pair_shifted, sems.at[0]))
        for u in range(SLOTS):
            made.append(put(swapped, pl.ds(0, SUB), u, column(swap_shifted, u), jnp.where(c == 0, 2, 0), swap_shifted, sems.at[0]))
        return made

    for n in range(8):
        @pl.when(role == n)
        def _():
            for m in copies(n):
                m.start()
            for m in copies(n):
                m.wait()

    @pl.when(last)
    def _():
        @pl.when(c == 0)
        def _():
            full[0, pl.ds(2 * SUB, SUB), :] = jnp.zeros((SUB, UNIT), jnp.float32)

        @pl.when(c == 1)
        def _():
            full[0, pl.ds(SUB, 2 * SUB), :] = jnp.zeros((2 * SUB, UNIT), jnp.float32)

    for t in range(STEPS):
        for u in range(SLOTS):
            value = full[u, pl.ds(t * SUB, SUB), :]
            top = value.astype(BF)
            high[pl.ds(t * SUB, SUB), pl.ds(u * UNIT, UNIT)] = top
            low[pl.ds(t * SUB, SUB), pl.ds(u * UNIT, UNIT)] = (value - top.astype(jnp.float32)).astype(BF)
    first = pl.ds(0, SUB)
    for t in range(STEPS):
        rows = pl.ds(t * SUB, SUB)
        out[0, t] = dot(high[first, :], high[rows, :]) + (
            dot(high[first, :], low[rows, :]) + dot(low[first, :], high[rows, :])
        )


def band(mains, tails, swapped):
    hbm = pl.BlockSpec(memory_space=pl.ANY)
    return pl.pallas_call(
        band_kernel,
        out_shape=jax.ShapeDtypeStruct((1, STEPS, SUB, SUB), jnp.float32),
        in_specs=[hbm] * 17,
        out_specs=pl.BlockSpec(memory_space=pltpu.VMEM),
        scratch_shapes=[
            pltpu.VMEM((SLOTS + 1, STEPS * SUB, UNIT), jnp.float32),
            pltpu.VMEM((STEPS * SUB, SLOTS * UNIT), BF),
            pltpu.VMEM((STEPS * SUB, SLOTS * UNIT), BF),
            pltpu.SemaphoreType.DMA((1,)),
        ],
    )(*mains, *tails, swapped)


def send(x, pairs):
    return lax.ppermute(x, ("row", "col"), pairs)


def shards(coeffs, pattern):
    head, tail = routes(main_of), routes(tail_of)
    lent = [(side_of(r), main_of(r)) for r in range(ROWS) if r % YS in (1, 2)]
    got_m, got_b = {}, {}

    def packed_head(p):
        return pack(coeffs, pattern, (p,), (0, 0, 0, 1), 3 * UNIT)

    def packed_tail(p, extra):
        return pack(coeffs, pattern, (p,), (2, 2, 2, 0), 2 * UNIT, extra)

    lend1 = send(pack(coeffs, pattern, (2, 3), (0, 3, 0, 0), UNIT), lent)
    lend2 = send(pack(coeffs, pattern, (1, 0), (0, 3, 0, 0), UNIT), lent)
    extra = {2: lend1[:PAIR], 3: lend1[PAIR:], 1: lend2[:PAIR], 0: lend2[PAIR:]}
    heads = {p: packed_head(p) for p in (2, 3, 1, 0)}
    tails = {p: packed_tail(p, extra[p]) for p in (2, 3, 1, 0)}
    for name in ("r1", "l1", "r2", "l2", "a0", "a1"):
        pair, moves = head[name]
        got_m[name] = send(heads[pair], moves)
        got_b[name] = send(tails[pair], tail[name][1])
    for name, via in (("f1", "r1"), ("f2", "l1")):
        got_m[name] = send(got_m[via], head[name][1])
        got_b[name] = send(got_b[via], head[name][1])
    mains, tails = [got_m[n] for n in ORDER], [got_b[n] for n in ORDER]
    mine = half(mains, tails)
    swapped = send(mine, [(i, i ^ 1) for i in range(ROWS * COLS)])
    return band(mains, tails, swapped)


def solution(mesh):
    in_specs = (P("row", "col"), P("row", "col"))
    out_specs = P(("row", "col"), None, None, None)
    return jax.shard_map(shards, mesh=mesh, in_specs=in_specs, out_specs=out_specs, check_vma=False)
```
